32 devices in a mesh: row: 8 (over z, core), col: 4 (over y, x).
Axes of the slice: x: 2, y: 2, z: 4, core: 2. Of those that a mesh axis runs over, the one named last changes fastest.
Arguments:
- ancestor: float32 [8, 1536, 12288], P(None, 'col', 'row'), may hold values from -6 to 6
- panels: float32 [2, 12288, 512], P(None, ('row', 'col')), may hold values from -0.06 to 0.06
- link_panels: float32 [1, 512, 512], P(None, 'row'), may hold values from -0.25 to 0.25
- diag_inverse: float32 [2, 512, 512], P(None, 'row'), may hold values from -0.25 to 0.25
- blocks: int32 [2, 48], replicated, may hold values from 0 to 95, as said below
Outputs:
- columns: float32 [2, 12288, 512], P(None, ('row', 'col'))
- diagonal: float32 [2, 512, 512], P(None, 'row', 'col')
The draws below stay inside these ranges and needn't reach their ends.
Inputs may be any that keep to these rules, and one draw needn't show every extreme that they name: Each of the 2 rows names 48 different row blocks.
All inputs are finite; a program needn't handle non-finite values.
Results may differ from the reference program's by a relative error of at most 0.0001.
Values sent between devices are 32-bit elements; how exact they have to be, the bound alone decides.
No kernel may reach another device: no remote copies, remote signals or barrier semaphores. Data moves between devices by JAX's collectives and lax.ppermute only.
A program may use at most 128 MiB of HBM per device.

```python
import jax
import jax.numpy as jnp
from jax import lax

M = 12288
W = 512
BLOCK = 128
NSUP = 2
SEL = 48
N_ROW = 8


def draw_blocks(key, part):
    rows_list = [jax.random.permutation(jax.random.fold_in(key, 17 + number), M // BLOCK)[:SEL] for number in range(NSUP)]
    return jnp.stack(rows_list).astype(jnp.int32)


def levels(key, shape, split, least, top_value):
    def one(dim, blocks):
        draws = jax.random.uniform(jax.random.fold_in(jax.random.fold_in(key, 6), dim), (blocks,), jnp.float32, least / len(split), top_value / len(split))
        return jnp.repeat(jnp.exp(draws), shape[dim] // blocks).reshape((-1,) + (1,) * (len(shape) - dim - 1))

    factor_of = one(*split[0])
    for cut in split[1:]:
        factor_of = factor_of * one(*cut)
    return factor_of


def normal_values(rng, dims, scale, reach, cuts=(), kind=jnp.bfloat16):
    loudness = levels(rng, dims, cuts, -0.22, 0.18) if cuts else 1.0
    result = jax.random.normal(rng, dims, jnp.float32) * scale * loudness
    return jnp.minimum(jnp.maximum(result, -reach), reach).astype(kind)


def setup_inputs(seed: int = 0) -> dict:
    streams_of = jax.random.split(jax.random.key(seed), 6)
    return {
        "ancestor": normal_values(streams_of[0], (N_ROW, M // N_ROW, M), 1.0, 6.0, ((1, 4), (2, 8)), jnp.float32),
        "panels": normal_values(streams_of[1], (NSUP, M, W), 0.01, 0.06, ((1, 32),), jnp.float32),
        "link_panels": normal_values(streams_of[2], (NSUP - 1, W, W), W ** -0.5, 0.25, ((1, 8),), jnp.float32),
        "diag_inverse": normal_values(streams_of[3], (NSUP, W, W), W ** -0.5, 0.25, ((1, 8),), jnp.float32),
        "blocks": draw_blocks(jax.random.fold_in(streams_of[5], 71), 0),
    }


def matmul(left, right):
    return jnp.dot(left, right, precision=lax.Precision.HIGHEST, preferred_element_type=jnp.float32)


def reference(ancestor, panels, link_panels, diag_inverse, blocks):
    whole = ancestor.reshape(M, M).T
    row_block = jnp.arange(M, dtype=jnp.int32) // BLOCK
    positions = jnp.arange(W, dtype=jnp.int32)
    lower_mask = positions[None, :] <= positions[:, None]
    col_list = []
    diag_list = []
    prev_cols = None
    prev_diag = None
    for supernode in range(NSUP):
        chosen = jnp.any(row_block[:, None] == blocks[supernode][None, :], axis=1)
        panel = jnp.where(chosen[:, None], panels[supernode], jnp.float32(0.0))
        product = matmul(whole, panel)
        lowered = jnp.where(lower_mask, diag_inverse[supernode], jnp.float32(0.0))
        gram = matmul(lowered.T, lowered)
        if supernode == 0:
            cols_now = -product
            diag_now = gram - matmul(panel.T, cols_now)
        else:
            link = link_panels[supernode - 1]
            carried = matmul(prev_cols, link)
            cols_now = -(product + carried)
            diag_now = gram - matmul(panel.T, cols_now) + matmul(carried.T, panel) + matmul(link.T, matmul(prev_diag, link))
        col_list.append(cols_now)
        diag_list.append(diag_now)
        prev_cols = cols_now
        prev_diag = diag_now
    return jnp.stack(col_list), jnp.stack(diag_list)
```

```python
import jax
import jax.numpy as jnp
from jax import lax
from jax.experimental import pallas as pl
from jax.experimental.pallas import tpu as pltpu
from jax.sharding import PartitionSpec as P

BLOCK = 128
LANES = 128
HIGH = lax.Precision.HIGH
F32 = jnp.float32
BF16 = jnp.bfloat16


def matmul(left, right):
    return jnp.dot(left, right, precision=HIGH, preferred_element_type=F32)


def matmul_left_t(left, right):
    return lax.dot_general(
        left, right, (((0,), (0,)), ((), ())), precision=HIGH, preferred_element_type=F32
    )


def select_rows(values, row_block, chosen):
    hit = jnp.any(row_block[:, None] == chosen[None, :], axis=1)
    return jnp.where(hit[:, None], values, jnp.float32(0.0))


def take(values, index, axis):
    return lax.dynamic_index_in_dim(values, index, axis, keepdims=False)


def split_two(values):
    high = values.astype(BF16)
    low = (values - high.astype(F32)).astype(BF16)
    return high, low


def product_kernel(count, line, parts, rows, picks, per_group, *refs):
    chosen_ref, place_ref, resident_ref = refs[:3]
    pieces = refs[3 : 3 + 2 * line * parts]
    outs = refs[3 + 2 * line * parts : 3 + 2 * line * parts + count]
    panel_ref, resident_buf, ids_ref, panel_sem, resident_sem = refs[-5:]
    place, core, col = place_ref[0], place_ref[1], place_ref[2]
    width = panel_ref.shape[1]
    part = width // parts
    copies = []
    for hop in range(line):
        source = (place + line - hop) % line
        for other in range(2):
            group = source * 2 + (core if other == 0 else 1 - core)
            for p in range(parts):
                copies.append(
                    pltpu.make_async_copy(
                        pieces[(hop * 2 + other) * parts + p].at[pl.ds(0, rows), :],
                        panel_ref.at[pl.ds(group * rows, rows), pl.ds(p * part, part)],
                        panel_sem.at[len(copies)],
                    )
                )
    for copy in copies:
        copy.start()

    def note(i, found):
        block = chosen_ref[i]
        group = block // per_group
        inner = block % per_group
        mine = inner // (rows // BLOCK) == col

        @pl.when(mine)
        def _():
            ids_ref[found] = group * (rows // BLOCK) + inner % (rows // BLOCK)

        return found + mine.astype(jnp.int32)

    found = lax.fori_loop(0, picks, note, jnp.int32(0))
    ids_ref[found] = ids_ref[jnp.maximum(found - 1, 0)]
    pairs = (found + 1) // 2

    def fetch(pair, slot):
        return [
            pltpu.make_async_copy(
                resident_ref.at[pl.ds(ids_ref[2 * pair + k] * BLOCK, BLOCK), :],
                resident_buf.at[slot, pl.ds(k * BLOCK, BLOCK), :],
                resident_sem.at[slot, k],
            )
            for k in range(2)
        ]

    @pl.when(pairs > 0)
    def _():
        for copy in fetch(0, 0):
            copy.start()

    for out in outs:
        out[...] = jnp.zeros(out.shape, F32)
    for copy in copies:
        copy.wait()

    def step(pair, carry):
        slot = pair % 2

        @pl.when(pair + 1 < pairs)
        def _():
            for copy in fetch(pair + 1, 1 - slot):
                copy.start()

        first = panel_ref[pl.ds(pl.multiple_of(ids_ref[2 * pair] * BLOCK, BLOCK), BLOCK), :]
        second = panel_ref[pl.ds(pl.multiple_of(ids_ref[2 * pair + 1] * BLOCK, BLOCK), BLOCK), :]
        second = jnp.where(2 * pair + 1 < found, second, jnp.float32(0.0))
        high, low = split_two(jnp.concatenate([first, second], axis=0))
        right = jnp.concatenate([high, low, high], axis=0)
        for copy in fetch(pair, slot):
            copy.wait()
        for j in range(count):
            start = pl.multiple_of((col ^ j) * rows, LANES)
            high, low = split_two(resident_buf[slot, :, pl.ds(start, rows)])
            left = jnp.concatenate([high, high, low], axis=0)
            outs[j][...] += lax.dot_general(
                left, right, (((0,), (0,)), ((), ())), preferred_element_type=F32
            )
        return carry

    lax.fori_loop(0, pairs, step, 0)


def fold(resident_t, pieces, parts, chosen, position, line, col_count):
    place, core, col = position
    rows = resident_t.shape[1] // col_count
    width = sum(piece.shape[1] for piece in pieces[0][0])
    if rows % LANES or rows % BLOCK:
        whole = jnp.zeros((line, 2, rows, width), F32)
        for hop in range(line):
            source = (place - hop) % line
            for other in range(2):
                value = jnp.concatenate(pieces[hop][other], axis=1)[:rows]
                side = core if other == 0 else 1 - core
                whole = lax.dynamic_update_slice(whole, value[None, None], (source, side, 0, 0))
        folded = matmul_left_t(resident_t, whole.reshape(-1, width))
        folded = folded.reshape(col_count, rows, width)
        return [take(folded, col ^ j, 0) for j in range(col_count)]
    flat = [piece for hop in pieces for side in hop for piece in side]
    picks = chosen.shape[0]
    per_group = rows * col_count // BLOCK

    def kernel(*refs):
        product_kernel(col_count, line, parts, rows, picks, per_group, *refs)

    smem = pl.BlockSpec(memory_space=pltpu.SMEM)
    hbm = pl.BlockSpec(memory_space=pl.ANY)
    return pl.pallas_call(
        kernel,
        out_shape=[jax.ShapeDtypeStruct((rows, width), F32)] * col_count,
        in_specs=[smem, smem, hbm] + [hbm] * len(flat),
        out_specs=[pl.BlockSpec(memory_space=pltpu.VMEM)] * col_count,
        scratch_shapes=[
            pltpu.VMEM((2 * line * rows, width), F32),
            pltpu.VMEM((2, 2 * BLOCK, resident_t.shape[1]), F32),
            pltpu.SMEM((picks + 2,), jnp.int32),
            pltpu.SemaphoreType.DMA((len(flat),)),
            pltpu.SemaphoreType.DMA((2, 2)),
        ],
        name="fold",
    )(chosen, jnp.stack(position).astype(jnp.int32), resident_t, *flat)


def body(ancestor, panels, link_panels, diag_inverse, blocks):
    row_count = lax.axis_size("row")
    col_count = lax.axis_size("col")
    row_index = lax.axis_index("row")
    col_index = lax.axis_index("col")
    line = row_count // 2
    place = row_index // 2
    core = row_index % 2
    resident_t = ancestor.reshape(ancestor.shape[0] * ancestor.shape[1], ancestor.shape[2])
    supernodes, rows_here, width = panels.shape
    rows_part = width // row_count
    cols_part = width // col_count
    share_rows = rows_part // col_count
    first_row = (row_index * col_count + col_index) * rows_here
    row_block = (first_row + jnp.arange(rows_here, dtype=jnp.int32)) // BLOCK
    swap = [(i, i ^ 1) for i in range(row_count)]

    def ring(hop):
        return [(i, (i + 2 * hop) % row_count) for i in range(row_count)]

    def near(j):
        return [(i, i ^ j) for i in range(col_count)]

    masked = [select_rows(panels[s], row_block, blocks[s]) for s in range(supernodes)]
    link_own = [
        lax.dynamic_slice_in_dim(link_panels[s], col_index * share_rows, share_rows, 0)
        for s in range(supernodes - 1)
    ]

    parts = 2
    part = width // parts
    position = (place, core, col_index)
    tie = lax.optimization_barrier

    def streams(s):
        values = []
        for p in range(parts):
            rows = [masked[s][:, p * part : (p + 1) * part]]
            if s + 1 < supernodes:
                rows.append(link_own[s][:, p * part : (p + 1) * part])
            values.append(jnp.concatenate(rows, axis=0))
        return values

    def both(values):
        return values, [lax.ppermute(value, "row", swap) for value in values]

    def shift(values):
        return [lax.ppermute(value, "row", ring(1)) for value in values]

    near_rows = [
        [masked[s]] + [lax.ppermute(masked[s], "col", near(j)) for j in range(1, col_count)]
        if s > 0
        else None
        for s in range(supernodes)
    ]
    near_rows = tuple(near_rows)

    gathered, folds = [], []
    ahead = streams(0)
    for s in range(supernodes):
        now = ahead
        hops = [both(now)]
        for hop in range(1, line):
            now = shift(now)
            if hop == 1 and s > 0:
                now, folds[s - 1] = tie((now, folds[s - 1]))
            hops.append(both(now))
            if hop == line - 2 and s + 1 < supernodes:
                ahead, _ = tie((streams(s + 1), now))
        if s + 1 < supernodes:
            hops, near_rows = tie((hops, near_rows))
        gathered.append(hops)
        folds.append(fold(resident_t, hops, parts, blocks[s], position, line, col_count))

    def link_whole(s):
        mine = jnp.zeros((line, 2, share_rows, width), F32)
        for hop in range(line):
            source = (place - hop) % line
            for other in range(2):
                value = jnp.concatenate([v[rows_here:] for v in gathered[s][hop][other]], axis=1)
                side = core if other == 0 else 1 - core
                mine = lax.dynamic_update_slice(mine, value[None, None], (source, side, 0, 0))
        mine = mine.reshape(row_count, 1, share_rows, width)
        whole = jnp.zeros((row_count, col_count, share_rows, width), F32)
        for j in range(col_count):
            value = mine if j == 0 else lax.ppermute(mine, "col", near(j))
            whole = lax.dynamic_update_slice(whole, value, (0, col_index ^ j, 0, 0))
        return whole.reshape(width, width)

    links = [link_whole(s) for s in range(supernodes - 1)]

    global_rows = row_index * rows_part + col_index * share_rows + jnp.arange(share_rows, dtype=jnp.int32)
    keep = jnp.arange(width, dtype=jnp.int32)[None, :] <= global_rows[:, None]

    def reduce_diag(partial):
        count = partial.shape[0]
        view = partial.reshape(count, line, 2, rows_part, width)
        theirs = take(view, 1 - core, 2)
        view = take(view, core, 2) + lax.ppermute(theirs, "row", swap)
        total = take(view, place, 1)
        for hop in range(1, line):
            target = (place + hop) % line
            total = total + lax.ppermute(take(view, target, 1), "row", ring(hop))
        view = total.reshape(count, rows_part, col_count, cols_part)
        total = take(view, col_index, 2)
        for j in range(1, col_count):
            total = total + lax.ppermute(take(view, col_index ^ j, 2), "col", near(j))
        return total

    col_list, partials = [], []
    for s in range(supernodes):
        folded = folds[s]
        slab = lax.dynamic_slice_in_dim(diag_inverse[s], col_index * share_rows, share_rows, 0)
        slab = jnp.where(keep, slab, jnp.float32(0.0))
        partial = matmul_left_t(slab, slab)
        product = folded[0]
        for j in range(1, col_count):
            product = product + lax.ppermute(folded[j], "col", near(j))
        if s == 0:
            cols_now = -product
            partial = partial - matmul_left_t(masked[s], cols_now)
        else:
            link = links[s - 1]
            carried = matmul(col_list[-1], link)
            cols_now = -(product + carried)
            partial = partial + matmul_left_t(carried, masked[s])
            partial = partial + matmul_left_t(masked[s], carried)
            partial = partial + matmul_left_t(link, matmul(partials[-1], link))
            for j in range(col_count):
                partial = partial + matmul_left_t(near_rows[s][j], folded[j])
        col_list.append(cols_now)
        partials.append(partial)
    return (jnp.stack(col_list), reduce_diag(jnp.stack(partials)))


def solution(mesh):
    placed = (
        P(None, "col", "row"),
        P(None, ("row", "col"), None),
        P(None, "row", None),
        P(None, "row", None),
        P(),
    )
    return jax.shard_map(
        body,
        mesh=mesh,
        in_specs=placed,
        out_specs=(P(None, ("row", "col"), None), P(None, "row", "col")),
        check_vma=False,
    )
```

```python
import jax
import jax.numpy as jnp
from jax import lax
from jax.experimental import pallas as pl
from jax.experimental.pallas import tpu as pltpu
from jax.sharding import PartitionSpec as P


BLOCK = 128
LANES = 128
HIGH = lax.Precision.HIGH
F32 = jnp.float32
BF16 = jnp.bfloat16


def matmul(left, right):
    return jnp.dot(left, right, precision=HIGH, preferred_element_type=F32)


def matmul_left_t(left, right):
    return lax.dot_general(
        left, right, (((0,), (0,)), ((), ())), precision=HIGH, preferred_element_type=F32
    )


def select_rows(values, row_block, chosen):
    hit = jnp.any(row_block[:, None] == chosen[None, :], axis=1)
    return jnp.where(hit[:, None], values, jnp.float32(0.0))


def take(values, index, axis):
    return lax.dynamic_index_in_dim(values, index, axis, keepdims=False)


def split_two(values):
    high = values.astype(BF16)
    low = (values - high.astype(F32)).astype(BF16)
    return high, low


def product_kernel(shape, *refs):
    count, line, first_hop, last_hop, parts, rows, picks, extra, seeded = shape
    per_group = rows * count // BLOCK
    per_device = rows // BLOCK
    inputs = 3 + 2 * (last_hop - first_hop) * parts
    chosen_ref, place_ref, resident_ref = refs[:3]
    pieces = refs[3:inputs]
    seeds = refs[inputs : inputs + count] if seeded else ()
    outs = refs[inputs + len(seeds) : inputs + len(seeds) + count]
    panel_ref, resident_buf, ids_ref, panel_sem, resident_sem, extra_sem = refs[-6:]
    place, core, col = place_ref[0], place_ref[1], place_ref[2]
    width = panel_ref.shape[1]
    part = width // parts

    def parts_of(hop, other):
        first = ((hop - first_hop) * 2 + other) * parts
        return pieces[first : first + parts]

    extras = []
    if extra:
        for hop in range(first_hop, last_hop):
            source = (place + line - hop) % line
            for other in range(2):
                group = source * 2 + (core if other == 0 else 1 - core)
                for p, piece in enumerate(parts_of(hop, other)):
                    extras.append(
                        pltpu.make_async_copy(
                            piece.at[pl.ds(rows, extra), :],
                            outs[0].at[pl.ds(rows + group * extra, extra), pl.ds(p * part, part)],
                            extra_sem.at[len(extras)],
                        )
                    )

    def panel_copy(piece, inner, slot, p):
        return pltpu.make_async_copy(
            piece.at[pl.ds(inner * BLOCK, BLOCK), :],
            panel_ref.at[pl.ds(slot * BLOCK, BLOCK), pl.ds(p * part, part)],
            panel_sem.at[slot, p],
        )

    def note(i, found):
        block = chosen_ref[i]
        group = block // per_group
        inner = block % per_group
        hop = (place + line - group // 2) % line
        mine = (inner // per_device == col) & (hop >= first_hop) & (hop < last_hop)

        @pl.when(mine)
        def _():
            ids_ref[found] = group * per_device + inner % per_device
            side = hop * 2 + jnp.where(group % 2 == core, 0, 1)
            for h in range(first_hop, last_hop):
                for other in range(2):

                    @pl.when(side == h * 2 + other)
                    def _():
                        for p, piece in enumerate(parts_of(h, other)):
                            panel_copy(piece, inner % per_device, found, p).start()

        return found + mine.astype(jnp.int32)

    found = lax.fori_loop(0, picks, note, jnp.int32(0))
    ids_ref[found] = ids_ref[jnp.maximum(found - 1, 0)]
    pairs = (found + 1) // 2

    def fetch(pair, slot):
        return [
            pltpu.make_async_copy(
                resident_ref.at[pl.ds(ids_ref[2 * pair + k] * BLOCK, BLOCK), :],
                resident_buf.at[slot, pl.ds(k * BLOCK, BLOCK), :],
                resident_sem.at[slot, k],
            )
            for k in range(2)
        ]

    @pl.when(pairs > 0)
    def _():
        for copy in fetch(0, 0):
            copy.start()

    for copy in extras:
        copy.start()
    for j, out in enumerate(outs):
        out[pl.ds(0, rows), :] = seeds[j][...] if seeded else jnp.zeros((rows, width), F32)

    def step(pair, carry):
        slot = pair % 2

        @pl.when(pair + 1 < pairs)
        def _():
            for copy in fetch(pair + 1, 1 - slot):
                copy.start()

        for p in range(parts):
            panel_copy(pieces[p], 0, 2 * pair, p).wait()

        @pl.when(2 * pair + 1 < found)
        def _():
            for p in range(parts):
                panel_copy(pieces[p], 0, 2 * pair + 1, p).wait()

        first = pl.multiple_of(pair * 2 * BLOCK, BLOCK)
        both = panel_ref[pl.ds(first, 2 * BLOCK), :]
        known = lax.broadcasted_iota(jnp.int32, both.shape, 0) < (found - 2 * pair) * BLOCK
        high, low = split_two(jnp.where(known, both, jnp.float32(0.0)))
        right = jnp.concatenate([high, low, high], axis=0)
        for copy in fetch(pair, slot):
            copy.wait()
        for j in range(count):
            start = pl.multiple_of((col ^ j) * rows, LANES)
            high, low = split_two(resident_buf[slot, :, pl.ds(start, rows)])
            left = jnp.concatenate([high, high, low], axis=0)
            outs[j][pl.ds(0, rows), :] += lax.dot_general(
                left, right, (((0,), (0,)), ((), ())), preferred_element_type=F32
            )
        return carry

    lax.fori_loop(0, pairs, step, 0)
    for copy in extras:
        copy.wait()
    if extra:
        for out in outs[1:]:
            out[pl.ds(rows, 2 * line * extra), :] = outs[0][pl.ds(rows, 2 * line * extra), :]


def terms_kernel(shape, *refs):
    count, line, rows, picks, share = shape
    chosen_ref, place_ref = refs[:2]
    panels = refs[2 : 2 + count]
    products = refs[2 + count : 2 + 2 * count]
    start_ref, mine_ref, other_ref = refs[2 + 2 * count : 5 + 2 * count]
    panel_ref, product_ref, total_ref, ids_ref, sems = refs[-5:]
    row, core, col = place_ref[0], place_ref[1], place_ref[2]
    per_group = rows * count // BLOCK
    per_device = rows // BLOCK
    copies = []
    for j in range(count):
        for k, (source, target) in enumerate(((panels[j], panel_ref), (products[j], product_ref))):
            copies.append(
                pltpu.make_async_copy(source, target.at[pl.ds(j * rows, rows), :], sems.at[j, k])
            )
    for copy in copies:
        copy.start()

    def note(i, found):
        block = chosen_ref[i]
        inner = block % per_group
        mine = block // per_group == row

        @pl.when(mine)
        def _():
            ids_ref[found] = ((inner // per_device) ^ col) * per_device + inner % per_device

        return found + mine.astype(jnp.int32)

    found = lax.fori_loop(0, picks, note, jnp.int32(0))
    ids_ref[found] = ids_ref[jnp.maximum(found - 1, 0)]
    total_ref[...] = start_ref[...]
    for copy in copies:
        copy.wait()

    def step(pair, carry):
        def both(ref):
            return jnp.concatenate(
                [
                    ref[pl.ds(pl.multiple_of(ids_ref[2 * pair + k] * BLOCK, BLOCK), BLOCK), :]
                    for k in range(2)
                ],
                axis=0,
            )

        value = both(panel_ref)
        known = lax.broadcasted_iota(jnp.int32, value.shape, 0) < (found - 2 * pair) * BLOCK
        high, low = split_two(jnp.where(known, value, jnp.float32(0.0)))
        left = jnp.concatenate([high, high, low], axis=0)
        high, low = split_two(both(product_ref))
        right = jnp.concatenate([high, low, high], axis=0)
        total_ref[...] += lax.dot_general(
            left, right, (((0,), (0,)), ((), ())), preferred_element_type=F32
        )
        return carry

    lax.fori_loop(0, (found + 1) // 2, step, 0)
    for place in range(line):
        for target, side in ((mine_ref, core), (other_ref, 1 - core)):
            first = pl.multiple_of((place * 2 + side) * share, 8)
            target[place] = total_ref[pl.ds(first, share), :]


def add_terms(panels, products, start, chosen, position, line):
    count = len(panels)
    rows, width = panels[0].shape
    share = width // (2 * line)
    picks = chosen.shape[0]
    smem = pl.BlockSpec(memory_space=pltpu.SMEM)
    hbm = pl.BlockSpec(memory_space=pl.ANY)
    vmem = pl.BlockSpec(memory_space=pltpu.VMEM)
    return pl.pallas_call(
        lambda *refs: terms_kernel((count, line, rows, picks, share), *refs),
        out_shape=[jax.ShapeDtypeStruct((line, share, width), F32)] * 2,
        in_specs=[smem, smem] + [hbm] * (2 * count) + [vmem],
        out_specs=[vmem] * 2,
        scratch_shapes=[
            pltpu.VMEM((count * rows, width), F32),
            pltpu.VMEM((count * rows, width), F32),
            pltpu.VMEM((width, width), F32),
            pltpu.SMEM((picks + 2,), jnp.int32),
            pltpu.SemaphoreType.DMA((count, 2)),
        ],
        name="terms",
    )(chosen, jnp.stack(position).astype(jnp.int32), *panels, *products, start)


def in_kernel(rows):
    return rows % LANES == 0 and rows % BLOCK == 0


def fold(resident_t, hops, first_hop, last_hop, parts, chosen, position, line, col_count, extra, seeds):
    rows = resident_t.shape[1] // col_count
    width = sum(piece.shape[1] for piece in hops[0][0])
    flat = [piece for hop in hops[first_hop:last_hop] for side in hop for piece in side]
    picks = chosen.shape[0]
    smem = pl.BlockSpec(memory_space=pltpu.SMEM)
    hbm = pl.BlockSpec(memory_space=pl.ANY)
    vmem = pl.BlockSpec(memory_space=pltpu.VMEM)
    seeds = list(seeds or ())
    shape = (col_count, line, first_hop, last_hop, parts, rows, picks, extra, bool(seeds))
    inputs = 3 + len(flat)
    blocks_here = 2 * line * rows // BLOCK
    return pl.pallas_call(
        lambda *refs: product_kernel(shape, *refs),
        out_shape=[jax.ShapeDtypeStruct((rows + 2 * line * extra, width), F32)] * col_count,
        in_specs=[smem, smem, hbm] + [hbm] * len(flat) + [vmem] * len(seeds),
        out_specs=[vmem] * col_count,
        input_output_aliases={inputs + j: j for j in range(len(seeds))},
        scratch_shapes=[
            pltpu.VMEM(((blocks_here + 2) * BLOCK, width), F32),
            pltpu.VMEM((2, 2 * BLOCK, resident_t.shape[1]), F32),
            pltpu.SMEM((picks + 2,), jnp.int32),
            pltpu.SemaphoreType.DMA((blocks_here + 2, parts)),
            pltpu.SemaphoreType.DMA((2, 2)),
            pltpu.SemaphoreType.DMA((len(flat),)),
        ],
        name="fold",
    )(chosen, jnp.stack(position).astype(jnp.int32), resident_t, *flat, *seeds)


def assemble(hops, position, line, first_row, rows):
    place, core, _ = position
    width = sum(piece.shape[1] for piece in hops[0][0])
    whole = jnp.zeros((line, 2, rows, width), F32)
    for hop in range(line):
        source = (place - hop) % line
        for other in range(2):
            value = jnp.concatenate(hops[hop][other], axis=1)[first_row : first_row + rows]
            side = core if other == 0 else 1 - core
            whole = lax.dynamic_update_slice(whole, value[None, None], (source, side, 0, 0))
    return whole.reshape(-1, width)


def fold_plain(resident_t, hops, position, line, col_count):
    rows = resident_t.shape[1] // col_count
    folded = matmul_left_t(resident_t, assemble(hops, position, line, 0, rows))
    folded = folded.reshape(col_count, rows, -1)
    return [take(folded, position[2] ^ j, 0) for j in range(col_count)]


def body(*arguments):
    fused = in_kernel(arguments[1].shape[1])
    return compute(fused, *arguments)


def compute(fused, ancestor, panels, link_panels, diag_inverse, blocks):
    row_count = lax.axis_size("row")
    col_count = lax.axis_size("col")
    row_index = lax.axis_index("row")
    col_index = lax.axis_index("col")
    line = row_count // 2
    place = row_index // 2
    core = row_index % 2
    resident_t = ancestor.reshape(ancestor.shape[0] * ancestor.shape[1], ancestor.shape[2])
    supernodes, rows_here, width = panels.shape
    rows_part = width // row_count
    cols_part = width // col_count
    share_rows = rows_part // col_count
    first_row = (row_index * col_count + col_index) * rows_here
    row_block = (first_row + jnp.arange(rows_here, dtype=jnp.int32)) // BLOCK
    swap = [(i, i ^ 1) for i in range(row_count)]

    def ring(hop):
        return [(i, (i + 2 * hop) % row_count) for i in range(row_count)]

    def near(j):
        return [(i, i ^ j) for i in range(col_count)]

    masked = [select_rows(panels[s], row_block, blocks[s]) for s in range(supernodes)]
    link_own = [
        lax.dynamic_slice_in_dim(link_panels[s], col_index * share_rows, share_rows, 0)
        for s in range(supernodes - 1)
    ]

    parts = 2
    part = width // parts
    position = (place, core, col_index)
    tie = lax.optimization_barrier if fused else lambda values: values

    def streams(s):
        values = []
        for p in range(parts):
            rows = [masked[s][:, p * part : (p + 1) * part]]
            if s + 1 < supernodes:
                rows.append(link_own[s][:, p * part : (p + 1) * part])
            values.append(jnp.concatenate(rows, axis=0))
        return values

    def both(values):
        return values, [lax.ppermute(value, "row", swap) for value in values]

    def shift(values):
        return [lax.ppermute(value, "row", ring(1)) for value in values]

    near_rows = [
        [masked[s]]
        + [lax.ppermute(masked[s], "col", near(j)) for j in range(1, col_count)]
        if s > 0
        else None
        for s in range(supernodes)
    ]
    near_rows = tuple(near_rows)

    global_rows = row_index * rows_part + col_index * share_rows + jnp.arange(share_rows, dtype=jnp.int32)
    keep = jnp.arange(width, dtype=jnp.int32)[None, :] <= global_rows[:, None]
    slabs = []
    for s in range(supernodes):
        slab = lax.dynamic_slice_in_dim(diag_inverse[s], col_index * share_rows, share_rows, 0)
        slab = jnp.where(keep, slab, jnp.float32(0.0))
        slabs.append(matmul_left_t(slab, slab))

    folds, products = [], []
    ahead = streams(0)
    for s in range(supernodes):
        last = s + 1 == supernodes
        extra = 0 if last else share_rows
        now = ahead
        hops = [both(now)]
        for hop in range(1, line):
            if hop > 1:
                now, hops[hop - 2] = tie((now, hops[hop - 2]))
            if hop == line - 1 and s == 0:
                now, slabs = tie((now, slabs))
            now = shift(now)
            if hop == 1 and s > 0:
                now, folds[s - 1] = tie((now, folds[s - 1]))
            if hop == line - 1 and last:
                hops, near_rows = tie((hops, near_rows))
                if fused:
                    made = fold(
                        resident_t, hops, 0, hop, parts, blocks[s], position, line, col_count, 0, None
                    )
                    now, made = tie((now, made))
            hops.append(both(now))
            if hop == line - 2 and not last:
                ahead, _ = tie((streams(s + 1), now))
        if fused:
            begin, seeds = (line - 1, made) if last and line > 1 else (0, None)
            made = fold(
                resident_t, hops, begin, line, parts, blocks[s], position, line, col_count, extra, seeds
            )
        else:
            made = fold_plain(resident_t, hops, position, line, col_count)
            if extra:
                tail = assemble(hops, position, line, rows_here, extra)
                made = [jnp.concatenate([value, tail], axis=0) for value in made]
        folds.append(made)
        products.append(
            [made[0]]
            + [lax.ppermute(made[j], "col", near(j)) for j in range(1, col_count)]
        )
    products[0], folds[-1] = tie((products[0], folds[-1]))

    def link_whole(s):
        whole = jnp.zeros((row_count, col_count, share_rows, width), F32)
        for j in range(col_count):
            value = products[s][j][rows_here:].reshape(row_count, 1, share_rows, width)
            whole = lax.dynamic_update_slice(whole, value, (0, col_index ^ j, 0, 0))
        return whole.reshape(width, width)

    links = [link_whole(s) for s in range(supernodes - 1)]

    def reduce_line(mine, theirs):
        view = mine + lax.ppermute(theirs, "row", swap)
        total = take(view, place, 0)
        for hop in range(1, line):
            target = (place + hop) % line
            total = total + lax.ppermute(take(view, target, 0), "row", ring(hop))
        return total

    def reduce_near(totals):
        view = totals.reshape(totals.shape[0], rows_part, col_count, cols_part)
        total = take(view, col_index, 2)
        for j in range(1, col_count):
            total = total + lax.ppermute(take(view, col_index ^ j, 2), "col", near(j))
        return total

    def by_core(partial):
        view = partial.reshape(line, 2, rows_part, width)
        return take(view, core, 1), take(view, 1 - core, 1)

    col_list, partials, totals = [], [], []
    for s in range(supernodes):
        partial = slabs[s]
        product = products[s][0]
        for j in range(1, col_count):
            product = product + products[s][j]
        product = product[:rows_here]
        if s == 0:
            cols_now = -product
            partial = partial - matmul_left_t(masked[s], cols_now)
        else:
            link = links[s - 1]
            carried = matmul(col_list[-1], link)
            cols_now = -(product + carried)
            partial = partial + matmul_left_t(carried, masked[s])
            partial = partial + matmul_left_t(masked[s], carried)
            partial = partial + matmul_left_t(link, matmul(partials[-1], link))
            if not fused:
                for j in range(col_count):
                    partial = partial + matmul_left_t(near_rows[s][j], folds[s][j])
        col_list.append(cols_now)
        partials.append(partial)
        if s > 0 and fused:
            sides = add_terms(
                near_rows[s], folds[s], partial, blocks[s], (row_index, core, col_index), line
            )
        else:
            sides = by_core(partial)
        totals.append(reduce_line(*sides))
    return (jnp.stack(col_list), reduce_near(jnp.stack(totals)))


def solution(mesh):
    placed = (
        P(None, "col", "row"),
        P(None, ("row", "col"), None),
        P(None, "row", None),
        P(None, "row", None),
        P(),
    )
    return jax.shard_map(
        body,
        mesh=mesh,
        in_specs=placed,
        out_specs=(P(None, ("row", "col"), None), P(None, "row", "col")),
        check_vma=False,
    )
```

```python
import jax
import jax.numpy as jnp
from jax import lax
from jax.experimental import pallas as pl
from jax.experimental.pallas import tpu as pltpu
from jax.sharding import PartitionSpec as P


BLOCK = 128
LANES = 128
HIGH = lax.Precision.HIGH
F32 = jnp.float32
BF16 = jnp.bfloat16


def matmul(left, right):
    return jnp.dot(left, right, precision=HIGH, preferred_element_type=F32)


def matmul_left_t(left, right):
    return lax.dot_general(
        left, right, (((0,), (0,)), ((), ())), precision=HIGH, preferred_element_type=F32
    )


def select_rows(values, row_block, chosen):
    hit = jnp.any(row_block[:, None] == chosen[None, :], axis=1)
    return jnp.where(hit[:, None], values, jnp.float32(0.0))


def take(values, index, axis):
    return lax.dynamic_index_in_dim(values, index, axis, keepdims=False)


def split_two(values):
    high = values.astype(BF16)
    low = (values - high.astype(F32)).astype(BF16)
    return high, low


def three_pass(left, right, left_dim, right_dim):
    left_high, left_low = split_two(left)
    right_high, right_low = split_two(right)
    return lax.dot_general(
        jnp.concatenate([left_high, left_high, left_low], axis=left_dim),
        jnp.concatenate([right_high, right_low, right_high], axis=right_dim),
        (((left_dim,), (right_dim,)), ((), ())),
        preferred_element_type=F32,
    )


def product_kernel(shape, *refs):
    count, line, first_hop, last_hop, parts, rows, extra, seeded = shape
    per_device = rows // BLOCK
    inputs = 3 + 2 * (last_hop - first_hop) * parts
    chosen_ref, place_ref, resident_ref = refs[:3]
    pieces = refs[3:inputs]
    seeds = refs[inputs : inputs + count] if seeded else ()
    outs = refs[inputs + len(seeds) : inputs + len(seeds) + count]
    panel_ref, resident_buf, ids_ref, panel_sem, resident_sem, extra_sem = refs[-6:]
    place, core, col = place_ref[0], place_ref[1], place_ref[2]
    width = panel_ref.shape[1]
    part = width // parts

    def parts_of(hop, other):
        first = ((hop - first_hop) * 2 + other) * parts
        return pieces[first : first + parts]

    extras = []
    if extra:
        for hop in range(first_hop, last_hop):
            source = (place + line - hop) % line
            for other in range(2):
                group = source * 2 + (core if other == 0 else 1 - core)
                for p, piece in enumerate(parts_of(hop, other)):
                    extras.append(
                        pltpu.make_async_copy(
                            piece.at[pl.ds(rows, extra), :],
                            outs[0].at[pl.ds(rows + group * extra, extra), pl.ds(p * part, part)],
                            extra_sem.at[len(extras)],
                        )
                    )

    def panel_copy(piece, inner, slot, p):
        return pltpu.make_async_copy(
            piece.at[pl.ds(inner * BLOCK, BLOCK), :],
            panel_ref.at[pl.ds(slot * BLOCK, BLOCK), pl.ds(p * part, part)],
            panel_sem.at[slot, p],
        )

    def note(hop, other, found):
        group = (place + line - hop) % line * 2 + (core if other == 0 else 1 - core)
        for inner in range(per_device):
            block = group * per_device + inner
            chosen = chosen_ref[block]

            @pl.when(chosen != 0)
            def _():
                ids_ref[found] = block
                for p, piece in enumerate(parts_of(hop, other)):
                    panel_copy(piece, inner, found, p).start()

            found = found + chosen
        return found

    found = jnp.int32(0)
    for hop in range(first_hop, last_hop):
        for other in range(2):
            found = note(hop, other, found)
    ids_ref[found] = ids_ref[jnp.maximum(found - 1, 0)]
    pairs = (found + 1) // 2

    def fetch(pair, slot):
        return [
            pltpu.make_async_copy(
                resident_ref.at[pl.ds(ids_ref[2 * pair + k] * BLOCK, BLOCK), :],
                resident_buf.at[slot, pl.ds(k * BLOCK, BLOCK), :],
                resident_sem.at[slot, k],
            )
            for k in range(2)
        ]

    @pl.when(pairs > 0)
    def _():
        for copy in fetch(0, 0):
            copy.start()

    for copy in extras:
        copy.start()
    for j, out in enumerate(outs):
        out[pl.ds(0, rows), :] = seeds[j][...] if seeded else jnp.zeros((rows, width), F32)

    def step(pair, carry):
        slot = pair % 2

        @pl.when(pair + 1 < pairs)
        def _():
            for copy in fetch(pair + 1, 1 - slot):
                copy.start()

        for p in range(parts):
            panel_copy(pieces[p], 0, 2 * pair, p).wait()

        @pl.when(2 * pair + 1 < found)
        def _():
            for p in range(parts):
                panel_copy(pieces[p], 0, 2 * pair + 1, p).wait()

        first = pl.multiple_of(pair * 2 * BLOCK, BLOCK)
        both = panel_ref[pl.ds(first, 2 * BLOCK), :]
        known = lax.broadcasted_iota(jnp.int32, both.shape, 0) < (found - 2 * pair) * BLOCK
        high, low = split_two(jnp.where(known, both, jnp.float32(0.0)))
        right = jnp.concatenate([high, low, high], axis=0)
        for copy in fetch(pair, slot):
            copy.wait()
        for j in range(count):
            start = pl.multiple_of((col ^ j) * rows, LANES)
            high, low = split_two(resident_buf[slot, :, pl.ds(start, rows)])
            left = jnp.concatenate([high, high, low], axis=0)
            outs[j][pl.ds(0, rows), :] += lax.dot_general(
                left, right, (((0,), (0,)), ((), ())), preferred_element_type=F32
            )
        return carry

    lax.fori_loop(0, pairs, step, 0)
    for copy in extras:
        copy.wait()
    if extra:
        for out in outs[1:]:
            out[pl.ds(rows, 2 * line * extra), :] = outs[0][pl.ds(rows, 2 * line * extra), :]


def part_by_core(total_ref, mine_ref, other_ref, line, core, share):
    for place in range(line):
        for target, side in ((mine_ref, core), (other_ref, 1 - core)):
            first = pl.multiple_of((place * 2 + side) * share, 8)
            target[place] = total_ref[pl.ds(first, share), :]


def columns_kernel(shape, *refs):
    count, line, rows, share = shape
    place_ref = refs[0]
    products = refs[1 : 1 + count]
    panel_ref, start_ref = refs[1 + count : 3 + count]
    columns_ref, link_ref, carried_ref, total_ref, mine_ref, other_ref = refs[3 + count :]
    core, col = place_ref[1], place_ref[2]
    extra = share // count
    for group in range(2 * line):
        for j in range(count):
            first = pl.multiple_of(group * share + (col ^ j) * extra, 8)
            link_ref[pl.ds(first, extra), :] = products[j][pl.ds(rows + group * extra, extra), :]
    columns = products[0][pl.ds(0, rows), :]
    for product in products[1:]:
        columns = columns + product[pl.ds(0, rows), :]
    columns = -columns
    columns_ref[...] = columns
    total_ref[...] = start_ref[...] - three_pass(panel_ref[...], columns, 0, 0)
    part_by_core(total_ref, mine_ref, other_ref, line, core, share)
    carried_ref[...] = three_pass(columns, link_ref[...], 1, 0)


def link_columns(products, panel, start, position, line):
    count = len(products)
    rows, width = panel.shape
    share = width // (2 * line)
    smem = pl.BlockSpec(memory_space=pltpu.SMEM)
    vmem = pl.BlockSpec(memory_space=pltpu.VMEM)
    shapes = [(rows, width), (width, width), (rows, width), (width, width)]
    shapes += [(line, share, width)] * 2
    return pl.pallas_call(
        lambda *refs: columns_kernel((count, line, rows, share), *refs),
        out_shape=[jax.ShapeDtypeStruct(shape, F32) for shape in shapes],
        in_specs=[smem] + [vmem] * (count + 2),
        out_specs=[vmem] * len(shapes),
        name="columns",
    )(position, *products, panel, start)


def terms_kernel(shape, *refs):
    count, line, rows, share = shape
    chosen_ref, place_ref = refs[:2]
    panels = refs[2 : 2 + count]
    products = refs[2 + count : 2 + 2 * count]
    start_ref, carried_ref, link_ref, before_ref, mine_ref, other_ref = refs[2 + 2 * count : 8 + 2 * count]
    panel_ref, product_ref, total_ref, sems = refs[-4:]
    core, col = place_ref[1], place_ref[2]
    per_device = rows // BLOCK
    own = pltpu.make_async_copy(
        panels[0], panel_ref.at[pl.ds(count * rows, rows), :], sems.at[2 * count * per_device]
    )
    own.start()

    def copies(j, inner, slot):
        return [
            pltpu.make_async_copy(
                source.at[pl.ds(inner * BLOCK, BLOCK), :],
                target.at[pl.ds(slot * BLOCK, BLOCK), :],
                sems.at[2 * slot + k],
            )
            for k, (source, target) in enumerate(((panels[j], panel_ref), (products[j], product_ref)))
        ]

    found = jnp.int32(0)
    for j in range(count):
        for inner in range(per_device):
            chosen = chosen_ref[(col ^ j) * per_device + inner]
            slot = found

            @pl.when(chosen != 0)
            def _():
                for copy in copies(j, inner, slot):
                    copy.start()

            found = found + chosen

    link = link_ref[...]
    linked = three_pass(link, three_pass(before_ref[...], link, 1, 0), 0, 0)
    total_ref[...] = start_ref[...] + linked
    own.wait()
    cross = three_pass(panel_ref[pl.ds(count * rows, rows), :], carried_ref[...], 0, 0)
    total_ref[...] += cross + cross.T

    def step(pair, carry):
        for copy in copies(0, 0, 2 * pair):
            copy.wait()

        @pl.when(2 * pair + 1 < found)
        def _():
            for copy in copies(0, 0, 2 * pair + 1):
                copy.wait()

        first = pl.multiple_of(pair * 2 * BLOCK, BLOCK)
        known = lax.broadcasted_iota(jnp.int32, (2 * BLOCK, 1), 0) < (found - 2 * pair) * BLOCK
        zero = jnp.float32(0.0)
        left = jnp.where(known, panel_ref[pl.ds(first, 2 * BLOCK), :], zero)
        right = jnp.where(known, product_ref[pl.ds(first, 2 * BLOCK), :], zero)
        total_ref[...] += three_pass(left, right, 0, 0)
        return carry

    lax.fori_loop(0, (found + 1) // 2, step, 0)
    part_by_core(total_ref, mine_ref, other_ref, line, core, share)


def add_terms(panels, products, start, carried, link, before, chosen, position, line):
    count = len(panels)
    rows, width = panels[0].shape
    share = width // (2 * line)
    smem = pl.BlockSpec(memory_space=pltpu.SMEM)
    hbm = pl.BlockSpec(memory_space=pl.ANY)
    vmem = pl.BlockSpec(memory_space=pltpu.VMEM)
    blocks_here = count * rows // BLOCK
    return pl.pallas_call(
        lambda *refs: terms_kernel((count, line, rows, share), *refs),
        out_shape=[jax.ShapeDtypeStruct((line, share, width), F32)] * 2,
        in_specs=[smem, smem] + [hbm] * (2 * count) + [vmem] * 4,
        out_specs=[vmem] * 2,
        scratch_shapes=[
            pltpu.VMEM(((count + 1) * rows + 2 * BLOCK, width), F32),
            pltpu.VMEM((count * rows + 2 * BLOCK, width), F32),
            pltpu.VMEM((width, width), F32),
            pltpu.SemaphoreType.DMA((2 * blocks_here + 3,)),
        ],
        name="terms",
    )(chosen, position, *panels, *products, start, carried, link, before)


def mark(value):
    hbm = pl.BlockSpec(memory_space=pl.ANY)
    return pl.pallas_call(
        lambda source, target: None,
        out_shape=jax.ShapeDtypeStruct(value.shape, value.dtype),
        in_specs=[hbm],
        out_specs=hbm,
        input_output_aliases={0: 0},
        name="mark",
    )(value)


def in_kernel(rows):
    return rows % LANES == 0 and rows % BLOCK == 0


def fold(resident_t, hops, first_hop, last_hop, parts, chosen, position, line, col_count, extra, seeds):
    rows = resident_t.shape[1] // col_count
    width = sum(piece.shape[1] for piece in hops[0][0])
    flat = [piece for hop in hops[first_hop:last_hop] for side in hop for piece in side]
    smem = pl.BlockSpec(memory_space=pltpu.SMEM)
    hbm = pl.BlockSpec(memory_space=pl.ANY)
    vmem = pl.BlockSpec(memory_space=pltpu.VMEM)
    seeds = list(seeds or ())
    shape = (col_count, line, first_hop, last_hop, parts, rows, extra, bool(seeds))
    inputs = 3 + len(flat)
    blocks_here = 2 * line * rows // BLOCK
    return pl.pallas_call(
        lambda *refs: product_kernel(shape, *refs),
        out_shape=[jax.ShapeDtypeStruct((rows + 2 * line * extra, width), F32)] * col_count,
        in_specs=[smem, smem, hbm] + [hbm] * len(flat) + [vmem] * len(seeds),
        out_specs=[vmem] * col_count,
        input_output_aliases={inputs + j: j for j in range(len(seeds))},
        scratch_shapes=[
            pltpu.VMEM(((blocks_here + 2) * BLOCK, width), F32),
            pltpu.VMEM((2, 2 * BLOCK, resident_t.shape[1]), F32),
            pltpu.SMEM((blocks_here + 2,), jnp.int32),
            pltpu.SemaphoreType.DMA((blocks_here + 2, parts)),
            pltpu.SemaphoreType.DMA((2, 2)),
            pltpu.SemaphoreType.DMA((len(flat),)),
        ],
        name="fold",
    )(chosen, position, resident_t, *flat, *seeds)


def assemble(hops, position, line, first_row, rows):
    place, core = position[0], position[1]
    width = sum(piece.shape[1] for piece in hops[0][0])
    whole = jnp.zeros((line, 2, rows, width), F32)
    for hop in range(line):
        source = (place - hop) % line
        for other in range(2):
            value = jnp.concatenate(hops[hop][other], axis=1)[first_row : first_row + rows]
            side = core if other == 0 else 1 - core
            whole = lax.dynamic_update_slice(whole, value[None, None], (source, side, 0, 0))
    return whole.reshape(-1, width)


def fold_plain(resident_t, hops, position, line, col_count):
    rows = resident_t.shape[1] // col_count
    folded = matmul_left_t(resident_t, assemble(hops, position, line, 0, rows))
    folded = folded.reshape(col_count, rows, -1)
    return [take(folded, position[2] ^ j, 0) for j in range(col_count)]


def body(*arguments):
    fused = in_kernel(arguments[1].shape[1])
    return compute(fused, *arguments)


def compute(fused, ancestor, panels, link_panels, diag_inverse, blocks):
    row_count = lax.axis_size("row")
    col_count = lax.axis_size("col")
    row_index = lax.axis_index("row")
    col_index = lax.axis_index("col")
    line = row_count // 2
    place = row_index // 2
    core = row_index % 2
    resident_t = ancestor.reshape(ancestor.shape[0] * ancestor.shape[1], ancestor.shape[2])
    supernodes, rows_here, width = panels.shape
    rows_part = width // row_count
    cols_part = width // col_count
    share_rows = rows_part // col_count
    first_row = (row_index * col_count + col_index) * rows_here
    row_block = (first_row + jnp.arange(rows_here, dtype=jnp.int32)) // BLOCK
    swap = [(i, i ^ 1) for i in range(row_count)]

    def ring(hop):
        return [(i, (i + 2 * hop) % row_count) for i in range(row_count)]

    def near(j):
        return [(i, i ^ j) for i in range(col_count)]

    masked = [select_rows(panels[s], row_block, blocks[s]) for s in range(supernodes)]
    link_own = [
        lax.dynamic_slice_in_dim(link_panels[s], col_index * share_rows, share_rows, 0)
        for s in range(supernodes - 1)
    ]

    tie = lax.optimization_barrier if fused else lambda values: values
    parts = 2
    part = width // parts
    position = jnp.stack([place, core, col_index]).astype(jnp.int32)
    blocks_per = max(rows_here // BLOCK, 1)
    hit = jnp.any(
        jnp.arange(row_count * col_count * blocks_per, dtype=jnp.int32)[None, :, None]
        == blocks[:, None, :],
        axis=2,
    ).astype(jnp.int32).reshape(supernodes, row_count, col_count, blocks_per)
    wanted = take(hit, col_index, 2).reshape(supernodes, -1)
    wanted_rows = take(hit, row_index, 1).reshape(supernodes, -1)
    wanted = [wanted[s] for s in range(supernodes)]
    wanted_rows = [wanted_rows[s] for s in range(supernodes)]
    position, wanted, wanted_rows = tie((position, wanted, wanted_rows))

    def streams(s):
        values = []
        for p in range(parts):
            rows = [masked[s][:, p * part : (p + 1) * part]]
            if s + 1 < supernodes:
                rows.append(link_own[s][:, p * part : (p + 1) * part])
            values.append(jnp.concatenate(rows, axis=0))
        return values

    def both(values):
        return values, [lax.ppermute(value, "row", swap) for value in values]

    def shift(values):
        return [lax.ppermute(value, "row", ring(1)) for value in values]

    near_rows = [
        [masked[s]]
        + [lax.ppermute(masked[s], "col", near(j)) for j in range(1, col_count)]
        if s > 0
        else None
        for s in range(supernodes)
    ]
    near_rows = tuple(near_rows)

    global_rows = row_index * rows_part + col_index * share_rows + jnp.arange(share_rows, dtype=jnp.int32)
    keep = jnp.arange(width, dtype=jnp.int32)[None, :] <= global_rows[:, None]
    slabs = []
    for s in range(supernodes):
        slab = lax.dynamic_slice_in_dim(diag_inverse[s], col_index * share_rows, share_rows, 0)
        slab = jnp.where(keep, slab, jnp.float32(0.0))
        slabs.append(matmul_left_t(slab, slab))

    folds, products = [], []
    ahead = streams(0)
    for s in range(supernodes):
        last = s + 1 == supernodes
        extra = 0 if last else share_rows
        now = ahead
        hops = [both(now)]
        for hop in range(1, line):
            if hop > 1:
                _, other = hops[hop - 2]
                for p in range(parts):
                    now[p], other[p] = tie((now[p], other[p]))
                    if fused:
                        other[p] = mark(other[p])
            if hop == line - 1 and s == 0:
                now[-1], slabs = tie((now[-1], slabs))
            now = shift(now)
            if hop == 1 and s > 0:
                for p in range(parts):
                    now[p], folds[s - 1][p] = tie((now[p], folds[s - 1][p]))
            if hop == line - 1 and last:
                hops, near_rows = tie((hops, near_rows))
                if fused:
                    made = fold(
                        resident_t, hops, 0, hop, parts, wanted[s], position, line, col_count, 0, None
                    )
                    made = list(made)
                    for p in range(parts):
                        now[p], made[p] = tie((now[p], made[p]))
            hops.append(both(now))
            if hop == line - 2 and not last:
                ahead = [tie((value, now[p]))[0] for p, value in enumerate(streams(s + 1))]
        if fused:
            begin, seeds = (line - 1, made) if last and line > 1 else (0, None)
            made = fold(
                resident_t, hops, begin, line, parts, wanted[s], position, line, col_count, extra, seeds
            )
        else:
            made = fold_plain(resident_t, hops, position, line, col_count)
            if extra:
                tail = assemble(hops, position, line, rows_here, extra)
                made = [jnp.concatenate([value, tail], axis=0) for value in made]
        folds.append(list(made))
        products.append(
            [made[0]]
            + [lax.ppermute(made[j], "col", near(j)) for j in range(1, col_count)]
        )
    products[0], folds[-1] = tie((products[0], folds[-1]))

    def link_whole(s):
        whole = jnp.zeros((row_count, col_count, share_rows, width), F32)
        for j in range(col_count):
            value = products[s][j][rows_here:].reshape(row_count, 1, share_rows, width)
            whole = lax.dynamic_update_slice(whole, value, (0, col_index ^ j, 0, 0))
        return whole.reshape(width, width)

    def reduce_line(mine, theirs):
        view = mine + lax.ppermute(theirs, "row", swap)
        total = take(view, place, 0)
        for hop in range(1, line):
            target = (place + hop) % line
            total = total + lax.ppermute(take(view, target, 0), "row", ring(hop))
        return total

    def reduce_near(totals):
        view = totals.reshape(totals.shape[0], rows_part, col_count, cols_part)
        total = take(view, col_index, 2)
        for j in range(1, col_count):
            total = total + lax.ppermute(take(view, col_index ^ j, 2), "col", near(j))
        return total

    def by_core(partial):
        view = partial.reshape(line, 2, rows_part, width)
        return take(view, core, 1), take(view, 1 - core, 1)

    if fused and supernodes == 2 and share_rows % 8 == 0:
        first, link, carried, before, mine, theirs = link_columns(
            products[0], masked[0], slabs[0], position, line
        )
        totals = [reduce_line(mine, theirs)]
        sides = add_terms(
            near_rows[1], folds[1], slabs[1], carried, link, before, wanted_rows[1], position, line
        )
        totals.append(reduce_line(*sides))
        product = products[1][0]
        for j in range(1, col_count):
            product = product + products[1][j]
        columns = jnp.stack([first, -(product + carried)])
        return (columns, reduce_near(jnp.stack(totals)))

    links = [link_whole(s) for s in range(supernodes - 1)]
    col_list, partials, totals = [], [], []
    for s in range(supernodes):
        partial = slabs[s]
        product = products[s][0]
        for j in range(1, col_count):
            product = product + products[s][j]
        product = product[:rows_here]
        if s == 0:
            cols_now = -product
            partial = partial - matmul_left_t(masked[s], cols_now)
        else:
            link = links[s - 1]
            carried = matmul(col_list[-1], link)
            cols_now = -(product + carried)
            partial = partial + matmul_left_t(carried, masked[s])
            partial = partial + matmul_left_t(masked[s], carried)
            partial = partial + matmul_left_t(link, matmul(partials[-1], link))
            for j in range(col_count):
                partial = partial + matmul_left_t(near_rows[s][j], folds[s][j])
        col_list.append(cols_now)
        partials.append(partial)
        totals.append(reduce_line(*by_core(partial)))
    return (jnp.stack(col_list), reduce_near(jnp.stack(totals)))


def solution(mesh):
    placed = (
        P(None, "col", "row"),
        P(None, ("row", "col"), None),
        P(None, "row", None),
        P(None, "row", None),
        P(),
    )
    return jax.shard_map(
        body,
        mesh=mesh,
        in_specs=placed,
        out_specs=(P(None, ("row", "col"), None), P(None, "row", "col")),
        check_vma=False,
    )
```
